32 devices in a mesh: context: 4 (over z), dp: 4 (over y, core), head: 2 (over x).
Axes of the slice: x: 2, y: 2, z: 4, core: 2. Of those that a mesh axis runs over, the one named last changes fastest.
Arguments:
- inputs: bfloat16 [4, 512, 2304], P('dp', 'context', 'head'), may hold values from -6 to 6
- output_grad: bfloat16 [4, 512, 2304], P('dp', 'context', 'head'), may hold values from -6 to 6
- qkv_weight: bfloat16 [2304, 3, 4096], P(None, None, 'head'), may hold values from -0.125 to 0.125
- out_weight: bfloat16 [2304, 4096], P(None, 'head'), may hold values from -0.09375 to 0.09375
- down_weight: bfloat16 [2304, 128], replicated, may hold values from -0.125 to 0.125
- up_weight: bfloat16 [128, 4096], P(None, 'head'), may hold values from -0.5 to 0.5
- beta_weight: bfloat16 [2304, 32], P(None, 'head'), may hold values from -0.125 to 0.125
- gate_bias: float32 [4096], P('head'), may hold values from -9 to -1.6, as said below
Outputs:
- layer_out: bfloat16 [4, 512, 2304], P('dp', 'context', 'head')
- input_grad: bfloat16 [4, 512, 2304], P('dp', 'context', 'head')
- qkv_grad: bfloat16 [2304, 3, 4096], P(('context', 'dp'), None, 'head')
- out_grad: bfloat16 [2304, 4096], P(('context', 'dp'), 'head')
- up_grad: float32 [128, 4096], P(None, 'head')
- down_grad: float32 [2304, 128], replicated
- beta_grad: float32 [2304, 32], P(None, 'head')
- bias_grad: float32 [4096], P('head')
The draws below stay inside these ranges and needn't reach their ends.
Inputs may be any that keep to these rules, and one draw needn't show every extreme that they name: `gate_bias`: offsets of the decay gate, one per channel.
All inputs are finite; a program needn't handle non-finite values.
Results may differ from the reference program's by a relative error of at most 0.02.
Values may be sent and summed in bfloat16 or wider, within the bound.
A program may use at most 192 MiB of HBM per device.

```python
import math
import jax
import jax.numpy as jnp
from jax import lax

D = 2304
H = 32
DK = 128
RANK = 128
SPAN = 64
TOK_DEV = 128
SEQS = 4
LENGTH = 512
N_HEAD = 2


def draw_gate_bias(key, part):
    choose_key, slow_key, fast_key = jax.random.split(key, 3)
    channels = H * DK
    fast_share = 0.5
    picked = jax.random.uniform(choose_key, (channels,), jnp.float32) < fast_share
    slow_rate = jnp.exp(jax.random.uniform(slow_key, (channels,), jnp.float32, math.log(0.3 / LENGTH), math.log(1.0 / LENGTH)))
    fast_rate = jnp.exp(jax.random.uniform(fast_key, (channels,), jnp.float32, math.log(1.0 / 60.0), math.log(1.0 / 25.0)))
    fraction = 4.0 * jnp.where(picked, fast_rate, slow_rate)
    return jnp.log(fraction / (1.0 - fraction)).astype(jnp.float32)


def block_scale(rng, extent, cuts, smallest, largest):
    factor_of = 1.0
    for position, parts in cuts:
        draws = jax.random.uniform(jax.random.fold_in(jax.random.fold_in(rng, 6), position), (parts,), jnp.float32, smallest / len(cuts), largest / len(cuts))
        factor_of = factor_of * jnp.repeat(jnp.exp(draws), extent[position] // parts).reshape((-1,) + (1,) * (len(extent) - 1 - position))
    return factor_of


def normal_values(stream_key, shape, width, reach, shards=(), kind=jnp.bfloat16):
    drawn = width * jax.random.normal(stream_key, shape, jnp.float32)
    if shards:
        drawn = drawn * block_scale(stream_key, shape, shards, -0.22, 0.18)
    return jnp.clip(drawn, -reach, reach).astype(kind)


def setup_inputs(seed: int = 0) -> dict:
    splits = jax.random.split(jax.random.key(seed), 9)
    inputs = normal_values(splits[0], (SEQS, LENGTH, D), 1.0, 6.0, ((0, 4), (1, 4), (2, 2)))
    output_grad = normal_values(splits[1], (SEQS, LENGTH, D), 1.0, 6.0, ((0, 4), (1, 4), (2, 2)))
    qkv_weight = normal_values(splits[2], (D, 3, H * DK), D ** -0.5, 0.125, ((2, 2),))
    out_weight = normal_values(splits[3], (D, H * DK), (H * DK) ** -0.5, 0.09375, ((1, 2),))
    down_weight = normal_values(splits[4], (D, RANK), D ** -0.5, 0.125)
    up_weight = normal_values(splits[5], (RANK, H * DK), RANK ** -0.5, 0.5, ((1, 2),))
    beta_weight = normal_values(splits[6], (D, H), D ** -0.5, 0.125, ((1, 2),))
    gate_bias = draw_gate_bias(jax.random.fold_in(splits[8], 71), 0)
    return dict(inputs=inputs, output_grad=output_grad, qkv_weight=qkv_weight, out_weight=out_weight, down_weight=down_weight, up_weight=up_weight, beta_weight=beta_weight, gate_bias=gate_bias)


epsilon = 1e-06
highest = lax.Precision.HIGHEST

def product(pattern, left, right):
    return jnp.einsum(pattern, left, right, precision=highest)

def dense(left, right):
    return jnp.dot(left.astype(jnp.float32), right.astype(jnp.float32), preferred_element_type=jnp.float32)

def activate(projected, gate_pre, beta_logit):
    token_count = projected.shape[0]
    head_count = beta_logit.shape[1]
    head_width = projected.shape[2] // head_count
    blocks = projected.reshape(token_count, 3, head_count, head_width)

    def normalize(values):
        return values * lax.rsqrt(lax.optimization_barrier(jnp.sum(values * values, axis=-1, keepdims=True)) + epsilon)
    queries = jnp.swapaxes(normalize(blocks[:, 0]), 0, 1)
    key_rows = jnp.swapaxes(normalize(blocks[:, 1]), 0, 1)
    value_rows = jnp.swapaxes(blocks[:, 2], 0, 1)
    decays = jnp.swapaxes((-0.25 * jax.nn.sigmoid(gate_pre)).reshape(token_count, head_count, head_width), 0, 1)
    betas = jnp.swapaxes(jax.nn.sigmoid(beta_logit), 0, 1)
    return (queries, key_rows, value_rows, decays, betas)

def span_terms(queries, key_rows, value_rows, decays, betas):
    leading = queries.shape[:-2]
    block_count = queries.shape[-2] // SPAN

    def blocked(member):
        return member.reshape(leading + (block_count, SPAN) + member.shape[-1:])
    queries, key_rows, value_rows, decays = (blocked(queries), blocked(key_rows), blocked(value_rows), blocked(decays))
    betas = betas.reshape(leading + (block_count, SPAN))
    cumulative = jnp.cumsum(decays, axis=-2)
    middle = cumulative[..., SPAN // 2 - 1:SPAN // 2, :]
    final_decay = cumulative[..., SPAN - 1:, :]
    key_fwd = jnp.exp(cumulative - middle) * key_rows
    key_back = jnp.exp(middle - cumulative) * key_rows
    query_fwd = jnp.exp(cumulative - middle) * queries
    key_start = jnp.exp(cumulative) * key_rows
    query_start = jnp.exp(cumulative) * queries
    key_end = jnp.exp(final_decay - cumulative) * key_rows
    row_index = lax.broadcasted_iota(jnp.int32, (SPAN, SPAN), 0)
    col_index = lax.broadcasted_iota(jnp.int32, (SPAN, SPAN), 1)
    strict = (row_index > col_index).astype(jnp.float32)
    lower_mask = (row_index >= col_index).astype(jnp.float32)
    coupling = betas[..., :, None] * product('...tc,...sc->...ts', key_fwd, key_back) * strict
    powers = -coupling
    inverse = jnp.eye(SPAN, dtype=jnp.float32) + powers
    for section in range(1, (SPAN - 1).bit_length()):
        powers = product('...ts,...su->...tu', powers, powers)
        inverse = inverse + product('...ts,...su->...tu', inverse, powers)
    solver = inverse * betas[..., None, :]
    solved_values = product('...ts,...sc->...tc', solver, value_rows)
    solved_keys = product('...ts,...sc->...tc', solver, key_start)
    scores = product('...tc,...sc->...ts', query_fwd, key_back) * lower_mask
    query_eff = query_start - product('...ts,...sc->...tc', scores, solved_keys)
    local_out = product('...ts,...sc->...tc', scores, solved_values)
    side = queries.shape[-1]
    diagonal = jnp.eye(side, dtype=jnp.float32) * jnp.exp(final_decay)[..., 0, :, None]
    transition = diagonal - product('...sc,...sd->...cd', key_end, solved_keys)
    offset = product('...sc,...sd->...cd', key_end, solved_values)
    return (query_eff, local_out, transition, offset)

def chain(terms, state_in):

    def advance(carried, pieces):
        query_eff, local_out, transition, offset = pieces
        emitted = product('...tc,...cd->...td', query_eff, carried) + local_out
        return (product('...cd,...de->...ce', transition, carried) + offset, emitted)
    moved = tuple((jnp.moveaxis(member, -3, 0) for member in terms))
    final_state, emitted = lax.scan(advance, state_in, moved)
    return (jnp.moveaxis(emitted, 0, -3), final_state)

def reference(inputs, output_grad, qkv_weight, out_weight, down_weight, up_weight, beta_weight, gate_bias):
    seq_count, seq_len, model_width = inputs.shape
    flat_in = inputs.reshape(-1, model_width)
    token_count = flat_in.shape[0]
    all_width = qkv_weight.shape[2]
    head_count = beta_weight.shape[1]
    head_width = all_width // head_count
    qkv_flat = qkv_weight.reshape(model_width, 3 * all_width)
    projected = dense(flat_in, qkv_flat).reshape(token_count, 3, all_width)
    low_rank = dense(flat_in, down_weight).astype(jnp.bfloat16)
    gate_pre = dense(low_rank, up_weight) + gate_bias
    beta_logit = dense(flat_in, beta_weight)
    acts, act_vjp = jax.vjp(activate, projected, gate_pre, beta_logit)

    def per_sequence(queries, key_rows, value_rows, decays, betas):
        shaped = [member.reshape((head_count, seq_count, seq_len) + member.shape[2:]) for member in (queries, key_rows, value_rows, decays, betas)]
        return span_terms(*shaped)
    terms, terms_vjp = jax.vjp(per_sequence, *acts)
    start_state = jnp.zeros((head_count, seq_count, head_width, head_width), jnp.float32)
    (mixed_blocks, final_state), chain_vjp = jax.vjp(chain, terms, start_state)
    mixed = jnp.transpose(mixed_blocks.reshape(head_count, seq_count, seq_len, head_width), (1, 2, 0, 3))
    mixed = mixed.reshape(token_count, all_width).astype(jnp.bfloat16)
    layer_out = dense(mixed, out_weight.T).astype(jnp.bfloat16).reshape(inputs.shape)
    flat_grad = output_grad.reshape(-1, model_width)
    mixed_grad = dense(flat_grad, out_weight)
    grad_blocks = jnp.transpose(mixed_grad.reshape(seq_count, seq_len, head_count, head_width), (2, 0, 1, 3))
    grad_blocks = grad_blocks.reshape(mixed_blocks.shape)
    term_grads, unused_state = chain_vjp((grad_blocks, jnp.zeros_like(final_state)))
    proj_grad, pre_grad, logit_grad = act_vjp(terms_vjp(term_grads))
    proj_low = proj_grad.astype(jnp.bfloat16).reshape(token_count, 3 * all_width)
    gate_low = pre_grad.astype(jnp.bfloat16)
    logit_low = logit_grad.astype(jnp.bfloat16)
    group_width = all_width // N_HEAD
    input_part = dense(proj_low, qkv_flat.T) + dense(logit_low, beta_weight.T)
    down_grad = jnp.zeros((model_width, down_weight.shape[1]), jnp.float32)
    for group in range(N_HEAD):
        low_grad = dense(gate_low[:, group * group_width:(group + 1) * group_width], up_weight[:, group * group_width:(group + 1) * group_width].T).astype(jnp.bfloat16)
        input_part = input_part + dense(low_grad, down_weight.T)
        down_grad = down_grad + dense(flat_in.T, low_grad)
    input_grad = input_part.astype(jnp.bfloat16).reshape(inputs.shape)
    block_total = token_count // TOK_DEV

    def block_rows(member):
        return member.reshape(block_total, TOK_DEV, member.shape[-1])
    stacked = (block_rows(flat_in), block_rows(proj_low), block_rows(flat_grad), block_rows(mixed))

    def accumulate(carried, pieces):
        input_rows, proj_rows, grad_rows, mixed_rows = pieces
        first = lax.optimization_barrier(dense(input_rows.T, proj_rows).astype(jnp.bfloat16)).astype(jnp.float32)
        second = lax.optimization_barrier(dense(grad_rows.T, mixed_rows).astype(jnp.bfloat16)).astype(jnp.float32)
        return ((carried[0] + first, carried[1] + second), None)
    start_sums = (jnp.zeros((model_width, 3 * all_width), jnp.float32), jnp.zeros((model_width, all_width), jnp.float32))
    (qkv_sum, out_sum), unused_rows = lax.scan(accumulate, start_sums, stacked)
    qkv_grad = qkv_sum.reshape(model_width, 3, all_width).astype(jnp.bfloat16)
    out_grad = out_sum.astype(jnp.bfloat16)
    up_grad = dense(low_rank.T, gate_low)
    beta_grad = dense(flat_in.T, logit_low)
    bias_grad = lax.optimization_barrier(jnp.sum(pre_grad, axis=0))
    return (layer_out, input_grad, qkv_grad, out_grad, up_grad, down_grad, beta_grad, bias_grad)
```

```python
import jax
import jax.numpy as jnp
from jax import lax
from jax.sharding import PartitionSpec as P

SPAN = 64


epsilon = 1e-06
highest = lax.Precision.HIGH


def shifted(value, axis, by):
    count = lax.axis_size(axis)
    pairs = [(i, i + by) for i in range(count) if 0 <= i + by < count]
    return lax.ppermute(value, axis, pairs)


def product(pattern, left, right):
    return jnp.einsum(pattern, left, right, precision=highest)


def activate(projected, gate_pre, beta_logit):
    token_count = projected.shape[0]
    head_count = beta_logit.shape[1]
    head_width = projected.shape[2] // head_count
    blocks = projected.reshape(token_count, 3, head_count, head_width)

    def normalize(values):
        return values * lax.rsqrt(jnp.sum(values * values, axis=-1, keepdims=True) + epsilon)

    queries = jnp.swapaxes(normalize(blocks[:, 0]), 0, 1)
    key_rows = jnp.swapaxes(normalize(blocks[:, 1]), 0, 1)
    value_rows = jnp.swapaxes(blocks[:, 2], 0, 1)
    decays = jnp.swapaxes(
        (-0.25 * jax.nn.sigmoid(gate_pre)).reshape(token_count, head_count, head_width), 0, 1
    )
    betas = jnp.swapaxes(jax.nn.sigmoid(beta_logit), 0, 1)
    return (queries, key_rows, value_rows, decays, betas)


def span_terms(queries, key_rows, value_rows, decays, betas):
    leading = queries.shape[:-2]
    block_count = queries.shape[-2] // SPAN

    def blocked(member):
        return member.reshape(leading + (block_count, SPAN) + member.shape[-1:])

    queries, key_rows, value_rows, decays = (
        blocked(queries),
        blocked(key_rows),
        blocked(value_rows),
        blocked(decays),
    )
    betas = betas.reshape(leading + (block_count, SPAN))
    cumulative = jnp.cumsum(decays, axis=-2)
    middle = cumulative[..., SPAN // 2 - 1 : SPAN // 2, :]
    final_decay = cumulative[..., SPAN - 1 :, :]
    key_fwd = jnp.exp(cumulative - middle) * key_rows
    key_back = jnp.exp(middle - cumulative) * key_rows
    query_fwd = jnp.exp(cumulative - middle) * queries
    key_start = jnp.exp(cumulative) * key_rows
    query_start = jnp.exp(cumulative) * queries
    key_end = jnp.exp(final_decay - cumulative) * key_rows
    row_index = lax.broadcasted_iota(jnp.int32, (SPAN, SPAN), 0)
    col_index = lax.broadcasted_iota(jnp.int32, (SPAN, SPAN), 1)
    strict = (row_index > col_index).astype(jnp.float32)
    lower_mask = (row_index >= col_index).astype(jnp.float32)
    coupling = betas[..., :, None] * product("...tc,...sc->...ts", key_fwd, key_back) * strict
    powers = -coupling
    inverse = jnp.eye(SPAN, dtype=jnp.float32) + powers
    for section in range(1, (SPAN - 1).bit_length()):
        powers = product("...ts,...su->...tu", powers, powers)
        inverse = inverse + product("...ts,...su->...tu", inverse, powers)
    solver = inverse * betas[..., None, :]
    solved_values = product("...ts,...sc->...tc", solver, value_rows)
    solved_keys = product("...ts,...sc->...tc", solver, key_start)
    scores = product("...tc,...sc->...ts", query_fwd, key_back) * lower_mask
    query_eff = query_start - product("...ts,...sc->...tc", scores, solved_keys)
    local_out = product("...ts,...sc->...tc", scores, solved_values)
    side = queries.shape[-1]
    diagonal = jnp.eye(side, dtype=jnp.float32) * jnp.exp(final_decay)[..., 0, :, None]
    transition = diagonal - product("...sc,...sd->...cd", key_end, solved_keys)
    offset = product("...sc,...sd->...cd", key_end, solved_values)
    return (query_eff, local_out, transition, offset)


def chain(terms, state_in):

    def chain_advance(carried, pieces):
        query_eff, local_out, transition, offset = pieces
        emitted = product("...tc,...cd->...td", query_eff, carried) + local_out
        return (product("...cd,...de->...ce", transition, carried) + offset, emitted)

    moved = tuple((jnp.moveaxis(member, -3, 0) for member in terms))
    final_state, emitted = lax.scan(chain_advance, state_in, moved)
    return (jnp.moveaxis(emitted, 0, -3), final_state)


def compose_spans(transition, offset, identity):

    def compose_advance(carried, pieces):
        return (
            (
                product("hcd,hde->hce", pieces[0], carried[0]),
                product("hcd,hde->hce", pieces[0], carried[1]) + pieces[1],
            ),
            None,
        )

    moved = (jnp.moveaxis(transition, -3, 0), jnp.moveaxis(offset, -3, 0))
    combined, unused_rows = lax.scan(compose_advance, (identity, jnp.zeros_like(identity)), moved)
    return combined


def shards(
    inputs, output_grad, qkv_weight, out_weight, down_weight, up_weight, beta_weight, gate_bias
):
    gathered = lax.all_gather(inputs, "head", axis=2, tiled=True)[0]
    token_count, model_width = gathered.shape
    all_width = qkv_weight.shape[2]
    head_count = beta_weight.shape[1]
    head_width = all_width // head_count
    qkv_flat = qkv_weight.reshape(model_width, 3 * all_width)
    projected = jnp.dot(gathered, qkv_flat, preferred_element_type=jnp.float32).reshape(
        token_count, 3, all_width
    )
    low_rank = jnp.dot(gathered, down_weight, preferred_element_type=jnp.float32).astype(
        jnp.bfloat16
    )
    gate_pre = jnp.dot(low_rank, up_weight, preferred_element_type=jnp.float32) + gate_bias
    beta_logit = jnp.dot(gathered, beta_weight, preferred_element_type=jnp.float32)
    acts, act_vjp = jax.vjp(activate, projected, gate_pre, beta_logit)
    terms, terms_vjp = jax.vjp(span_terms, *acts)
    identity = jnp.broadcast_to(
        jnp.eye(head_width, dtype=jnp.float32), (head_count, head_width, head_width)
    )
    empty = jnp.zeros((head_count, head_width, head_width), jnp.float32)
    shard_linear, shard_offset = compose_spans(terms[2], terms[3], identity)

    grad_whole = lax.all_gather(output_grad, "head", axis=2, tiled=True)[0]
    mixed_grad = jnp.dot(grad_whole, out_weight, preferred_element_type=jnp.float32)
    grad_blocks = jnp.swapaxes(
        mixed_grad.reshape(token_count, head_count, head_width), 0, 1
    ).reshape(terms[1].shape)
    own_grad = jnp.zeros_like(empty)
    for block in reversed(range(token_count // SPAN)):
        own_grad = product("hcd,hce->hde", terms[2][:, block], own_grad) + product(
            "htc,htd->hcd", terms[0][:, block], grad_blocks[:, block]
        )
    linear_back = jnp.swapaxes(shard_linear, 1, 2)
    shard_count = lax.axis_size("context")
    shard_index = lax.axis_index("context")
    state_in, state_grad = empty, empty
    for step in range(shard_count - 1):
        leaving = shard_offset
        leaving_grad = own_grad
        if step:
            leaving = product("hcd,hde->hce", shard_linear, state_in) + leaving
            leaving_grad = product("hcd,hde->hce", linear_back, state_grad) + leaving_grad
        state_in = shifted(leaving.astype(jnp.bfloat16), "context", 1).astype(jnp.float32)
        state_grad = shifted(leaving_grad.astype(jnp.bfloat16), "context", -1).astype(jnp.float32)
    (mixed_blocks, final_state), chain_vjp = jax.vjp(chain, terms, state_in)
    mixed = jnp.swapaxes(mixed_blocks.reshape(head_count, token_count, head_width), 0, 1)
    mixed = mixed.reshape(token_count, all_width).astype(jnp.bfloat16)
    slab = model_width // shard_count

    def slab_of(member):
        whole = lax.all_gather(member, "context", axis=0, tiled=True)
        return lax.dynamic_slice_in_dim(whole, shard_index * slab, slab, axis=1)

    def weight_term(rows, columns):
        whole = lax.all_gather(columns, "context", axis=0, tiled=True)
        term = jnp.einsum("tr,tc->rc", rows, whole, preferred_element_type=jnp.float32)
        return lax.psum_scatter(
            term.astype(jnp.bfloat16), "dp", scatter_dimension=0, tiled=True
        )

    input_slab = slab_of(gathered)
    grad_slab = slab_of(grad_whole)
    out_grad = weight_term(grad_slab, mixed)
    out_part = jnp.einsum("tc,dc->td", mixed, out_weight, preferred_element_type=jnp.float32)
    layer_out = lax.psum_scatter(
        out_part.astype(jnp.bfloat16), "head", scatter_dimension=1, tiled=True
    )[None]
    term_grads, unused_state = chain_vjp((grad_blocks, state_grad))
    proj_grad, pre_grad, logit_grad = act_vjp(terms_vjp(term_grads))
    proj_parts = [proj_grad[:, part].astype(jnp.bfloat16) for part in range(3)]
    qkv_grad = jnp.stack([weight_term(input_slab, part) for part in proj_parts], axis=1)
    gate_low = pre_grad.astype(jnp.bfloat16)
    logit_low = logit_grad.astype(jnp.bfloat16)
    low_grad = jnp.einsum(
        "tc,rc->tr", gate_low, up_weight, preferred_element_type=jnp.float32
    ).astype(jnp.bfloat16)
    up_term = jnp.einsum("tr,tc->rc", low_rank, gate_low, preferred_element_type=jnp.float32)
    beta_term = jnp.einsum("td,th->dh", gathered, logit_low, preferred_element_type=jnp.float32)
    bias_term = jnp.sum(pre_grad, axis=0)
    down_term = jnp.einsum("td,tr->dr", gathered, low_grad, preferred_element_type=jnp.float32)
    small = [up_term, down_term, beta_term, bias_term]
    packed = jnp.concatenate([term.astype(jnp.bfloat16).reshape(-1, 128) for term in small], axis=0)
    packed = lax.psum(packed, ("context", "dp")).astype(jnp.float32)
    results, start = [], 0
    for term in small:
        count = term.size // 128
        results.append(packed[start : start + count].reshape(term.shape))
        start += count
    up_grad, down_grad, beta_grad, bias_grad = results
    down_grad = lax.psum(down_grad, "head")
    input_part = jnp.einsum(
        "tr,dr->td", low_grad, down_weight, preferred_element_type=jnp.float32
    )
    input_part = input_part + jnp.einsum(
        "th,dh->td", logit_low, beta_weight, preferred_element_type=jnp.float32
    )
    input_part = input_part + jnp.einsum(
        "tc,dc->td",
        jnp.concatenate(proj_parts, axis=1),
        qkv_flat,
        preferred_element_type=jnp.float32,
    )
    input_grad = lax.psum_scatter(
        input_part.astype(jnp.bfloat16), "head", scatter_dimension=1, tiled=True
    )[None]
    return (layer_out, input_grad, qkv_grad, out_grad, up_grad, down_grad, beta_grad, bias_grad)


def solution(mesh):
    return jax.shard_map(
        shards,
        mesh=mesh,
        in_specs=(
            P("dp", "context", "head"),
            P("dp", "context", "head"),
            P(None, None, "head"),
            P(None, "head"),
            P(),
            P(None, "head"),
            P(None, "head"),
            P("head"),
        ),
        out_specs=(
            P("dp", "context", "head"),
            P("dp", "context", "head"),
            P(("context", "dp"), None, "head"),
            P(("context", "dp"), "head"),
            P(None, "head"),
            P(),
            P(None, "head"),
            P("head"),
        ),
        check_vma=False,
    )
```

```python
import jax
import jax.numpy as jnp
from jax import lax
from jax.experimental import pallas as pl
from jax.experimental.pallas import tpu as pltpu
from jax.sharding import PartitionSpec as P

SPAN = 64


epsilon = 1e-06
highest = lax.Precision.HIGH


def shifted(value, axis, by):
    count = lax.axis_size(axis)
    pairs = [(i, i + by) for i in range(count) if 0 <= i + by < count]
    return lax.ppermute(value, axis, pairs)


def product(pattern, left, right):
    return jnp.einsum(pattern, left, right, precision=highest)


def halves(value):
    high = value.astype(jnp.bfloat16)
    return high, (value - high.astype(jnp.float32)).astype(jnp.bfloat16)


def multiply(left, right, left_dim, right_dim):
    def one(first, second):
        return lax.dot_general(
            first,
            second,
            (((left_dim,), (right_dim,)), ((), ())),
            preferred_element_type=jnp.float32,
        )

    left_high, left_low = halves(left)
    right_high, right_low = halves(right)
    return (one(left_high, right_low) + one(left_low, right_high)) + one(left_high, right_high)


@jax.custom_vjp
def mat_nn(left, right):
    return multiply(left, right, 1, 0)


@jax.custom_vjp
def mat_nt(left, right):
    return multiply(left, right, 1, 1)


@jax.custom_vjp
def mat_tn(left, right):
    return multiply(left, right, 0, 0)


def keep(function):
    return lambda left, right: (function(left, right), (left, right))


mat_nn.defvjp(
    keep(mat_nn), lambda kept, grad: (mat_nt(grad, kept[1]), mat_tn(kept[0], grad))
)
mat_nt.defvjp(
    keep(mat_nt), lambda kept, grad: (mat_nn(grad, kept[1]), mat_tn(grad, kept[0]))
)
mat_tn.defvjp(
    keep(mat_tn), lambda kept, grad: (mat_nt(kept[1], grad), mat_nn(kept[0], grad))
)


def identity_of(side):
    row_index = lax.broadcasted_iota(jnp.int32, (side, side), 0)
    col_index = lax.broadcasted_iota(jnp.int32, (side, side), 1)
    return (row_index == col_index).astype(jnp.float32)


@jax.custom_vjp
def unit_inverse(coupling):
    powers = -coupling
    inverse = identity_of(SPAN) + powers
    for section in range(1, (SPAN - 1).bit_length()):
        powers = mat_nn(powers, powers)
        inverse = inverse + mat_nn(inverse, powers)
    return inverse


def inverse_forward(coupling):
    inverse = unit_inverse(coupling)
    return inverse, inverse


def inverse_backward(inverse, grad):
    return (-mat_nt(mat_tn(inverse, grad), inverse),)


unit_inverse.defvjp(inverse_forward, inverse_backward)


def block_terms(query_raw, key_raw, value_rows, gate, beta_raw):
    def normalize(values):
        return values * lax.rsqrt(jnp.sum(values * values, axis=-1, keepdims=True) + epsilon)

    queries, key_rows = normalize(query_raw), normalize(key_raw)
    decays = -0.25 * lax.logistic(gate)
    betas = lax.logistic(beta_raw)
    row_index = lax.broadcasted_iota(jnp.int32, (SPAN, SPAN), 0)
    col_index = lax.broadcasted_iota(jnp.int32, (SPAN, SPAN), 1)
    strict = (row_index > col_index).astype(jnp.float32)
    lower_mask = (row_index >= col_index).astype(jnp.float32)
    wide_index = lax.broadcasted_iota(jnp.int32, decays.shape, 0)
    cumulative = mat_nn(lower_mask, decays)
    middle = lax.stop_gradient(
        jnp.sum(jnp.where(wide_index < SPAN // 2, decays, 0.0), axis=0, keepdims=True)
    )
    final_decay = jnp.sum(decays, axis=0, keepdims=True)
    grow = jnp.exp(cumulative - middle)
    start = jnp.exp(cumulative)
    key_fwd = grow * key_rows
    key_back = jnp.exp(middle - cumulative) * key_rows
    query_fwd = grow * queries
    key_start = start * key_rows
    query_start = start * queries
    key_end = jnp.exp(final_decay - cumulative) * key_rows
    coupling = betas * mat_nt(key_fwd, key_back) * strict
    inverse = unit_inverse(coupling)
    solved_values = mat_nn(inverse, betas * value_rows)
    solved_keys = mat_nn(inverse, betas * key_start)
    scores = mat_nt(query_fwd, key_back) * lower_mask
    query_eff = query_start - mat_nn(scores, solved_keys)
    local_out = mat_nn(scores, solved_values)
    transition = identity_of(gate.shape[1]) * jnp.exp(final_decay) - mat_tn(key_end, solved_keys)
    offset = mat_tn(key_end, solved_values)
    return query_eff, local_out, transition, offset


def run_blocks(pieces, state):
    emitted = []
    for piece in pieces:
        query_eff, local_out, transition, offset = block_terms(*piece)
        emitted.append(mat_nn(query_eff, state) + local_out)
        state = mat_nn(transition, state) + offset
    return emitted, state


def head_pieces(refs, part, width, head):
    columns = slice(part * width, (part + 1) * width)
    logits = refs[4][...]
    picked = lax.broadcasted_iota(jnp.int32, logits.shape, 1) == head
    beta_raw = jnp.sum(jnp.where(picked, logits, 0.0), axis=1, keepdims=True)
    pieces = []
    for block in range(logits.shape[0] // SPAN):
        rows = slice(block * SPAN, (block + 1) * SPAN)
        pieces.append(tuple(ref[rows, columns] for ref in refs[:4]) + (beta_raw[rows],))
    return pieces, columns, picked


def summary_kernel(*refs):
    grad_ref, linear_ref, offset_ref, own_ref = refs[5:]
    together, width = linear_ref.shape[0], linear_ref.shape[1]
    for part in range(together):
        head = pl.program_id(0) * together + part
        pieces, columns, picked = head_pieces(refs, part, width, head)
        terms = [block_terms(*piece) for piece in pieces]
        linear, total = terms[0][2], terms[0][3]
        for term in terms[1:]:
            linear = mat_nn(term[2], linear)
            total = mat_nn(term[2], total) + term[3]
        own = None
        for block in reversed(range(len(terms))):
            rows = slice(block * SPAN, (block + 1) * SPAN)
            local = mat_tn(terms[block][0], grad_ref[rows, columns])
            own = local if own is None else mat_tn(terms[block][2], own) + local
        linear_ref[part] = linear
        offset_ref[part] = total
        own_ref[part] = own


def gradient_kernel(*refs):
    grad_ref, state_ref, after_ref = refs[5:8]
    mixed_ref, query_ref, key_ref, value_ref, gate_ref, bias_ref, logit_ref = refs[8:]
    together, width = state_ref.shape[0], state_ref.shape[1]

    @pl.when(pl.program_id(0) == 0)
    def clear():
        logit_ref[...] = jnp.zeros_like(logit_ref)

    for part in range(together):
        head = pl.program_id(0) * together + part
        pieces, columns, picked = head_pieces(refs, part, width, head)
        state = state_ref[part]
        outs, pull = jax.vjp(lambda given: run_blocks(given, state), pieces)
        count = len(pieces)
        grads = [grad_ref[slice(n * SPAN, (n + 1) * SPAN), columns] for n in range(count)]
        (piece_grads,) = pull((grads, after_ref[part]))
        bias = jnp.zeros((1, width), jnp.float32)
        for block in range(count):
            rows = slice(block * SPAN, (block + 1) * SPAN)
            query_grad, key_grad, value_grad, gate_grad, beta_grad = piece_grads[block]
            mixed_ref[rows, columns] = outs[0][block].astype(jnp.bfloat16)
            query_ref[rows, columns] = query_grad.astype(jnp.bfloat16)
            key_ref[rows, columns] = key_grad.astype(jnp.bfloat16)
            value_ref[rows, columns] = value_grad.astype(jnp.bfloat16)
            gate_ref[rows, columns] = gate_grad.astype(jnp.bfloat16)
            bias = bias + jnp.sum(gate_grad, axis=0, keepdims=True)
            logit_ref[rows, :] += jnp.where(picked[rows], beta_grad, 0.0)
        bias_ref[:, columns] = bias


def head_calls(projected, gate_pre, beta_logit, mixed_grad, together=2):
    token_count, all_width = gate_pre.shape
    head_count = beta_logit.shape[1]
    width = all_width // head_count
    steps = head_count // together

    def column(shift):
        return pl.BlockSpec((token_count, together * width), lambda step: (0, step + shift * steps))

    whole = pl.BlockSpec((token_count, head_count), lambda step: (0, 0))
    states = pl.BlockSpec((together, width, width), lambda step: (step, 0, 0))
    state_shape = jax.ShapeDtypeStruct((head_count, width, width), jnp.float32)
    wide_shape = jax.ShapeDtypeStruct((token_count, all_width), jnp.bfloat16)
    common = [column(0), column(1), column(2), column(0), whole, column(0)]
    given = (projected, projected, projected, gate_pre, beta_logit, mixed_grad)
    params = pltpu.CompilerParams(vmem_limit_bytes=48 * 1024 * 1024)

    def summary():
        return pl.pallas_call(
            summary_kernel,
            grid=(steps,),
            in_specs=common,
            out_specs=[states] * 3,
            out_shape=[state_shape] * 3,
            compiler_params=params,
        )(*given)

    def gradient(state_in, state_grad):
        return pl.pallas_call(
            gradient_kernel,
            grid=(steps,),
            in_specs=common + [states, states],
            out_specs=[column(0)] * 5
            + [pl.BlockSpec((1, together * width), lambda step: (0, step)), whole],
            out_shape=[wide_shape] * 5
            + [
                jax.ShapeDtypeStruct((1, all_width), jnp.float32),
                jax.ShapeDtypeStruct((token_count, head_count), jnp.float32),
            ],
            compiler_params=params,
        )(*given, state_in, state_grad)

    return summary, gradient


def shards(
    inputs, output_grad, qkv_weight, out_weight, down_weight, up_weight, beta_weight, gate_bias
):
    gathered = lax.all_gather(inputs, "head", axis=2, tiled=True)[0]
    token_count, model_width = gathered.shape
    all_width = qkv_weight.shape[2]
    head_count = beta_weight.shape[1]
    head_width = all_width // head_count
    qkv_flat = qkv_weight.reshape(model_width, 3 * all_width)
    projected = jnp.dot(gathered, qkv_flat, preferred_element_type=jnp.float32)
    low_rank = jnp.dot(gathered, down_weight, preferred_element_type=jnp.float32).astype(
        jnp.bfloat16
    )
    gate_pre = jnp.dot(low_rank, up_weight, preferred_element_type=jnp.float32) + gate_bias
    beta_logit = jnp.dot(gathered, beta_weight, preferred_element_type=jnp.float32)
    empty = jnp.zeros((head_count, head_width, head_width), jnp.float32)
    grad_whole = lax.all_gather(output_grad, "head", axis=2, tiled=True)[0]
    mixed_grad = jnp.dot(grad_whole, out_weight, preferred_element_type=jnp.float32)
    summary, gradient = head_calls(projected, gate_pre, beta_logit, mixed_grad)
    shard_linear, shard_offset, own_grad = summary()
    linear_back = jnp.swapaxes(shard_linear, 1, 2)
    shard_count = lax.axis_size("context")
    shard_index = lax.axis_index("context")
    state_in, state_grad = empty, empty
    for step in range(shard_count - 1):
        leaving = shard_offset
        leaving_grad = own_grad
        if step:
            leaving = product("hcd,hde->hce", shard_linear, state_in) + leaving
            leaving_grad = product("hcd,hde->hce", linear_back, state_grad) + leaving_grad
        state_in = shifted(leaving.astype(jnp.bfloat16), "context", 1).astype(jnp.float32)
        state_grad = shifted(leaving_grad.astype(jnp.bfloat16), "context", -1).astype(jnp.float32)
    mixed, *proj_parts, gate_low, bias_term, logit_grad = gradient(state_in, state_grad)
    slab = model_width // shard_count

    def slab_of(member):
        whole = lax.all_gather(member, "context", axis=0, tiled=True)
        return lax.dynamic_slice_in_dim(whole, shard_index * slab, slab, axis=1)

    def weight_term(rows, columns):
        whole = lax.all_gather(columns, "context", axis=0, tiled=True)
        term = jnp.einsum("tr,tc->rc", rows, whole, preferred_element_type=jnp.float32)
        return lax.psum_scatter(
            term.astype(jnp.bfloat16), "dp", scatter_dimension=0, tiled=True
        )

    input_slab = slab_of(gathered)
    grad_slab = slab_of(grad_whole)
    out_grad = weight_term(grad_slab, mixed)
    out_part = jnp.einsum("tc,dc->td", mixed, out_weight, preferred_element_type=jnp.float32)
    layer_out = lax.psum_scatter(
        out_part.astype(jnp.bfloat16), "head", scatter_dimension=1, tiled=True
    )[None]
    qkv_grad = jnp.stack([weight_term(input_slab, part) for part in proj_parts], axis=1)
    logit_low = logit_grad.astype(jnp.bfloat16)
    low_grad = jnp.einsum(
        "tc,rc->tr", gate_low, up_weight, preferred_element_type=jnp.float32
    ).astype(jnp.bfloat16)
    up_term = jnp.einsum("tr,tc->rc", low_rank, gate_low, preferred_element_type=jnp.float32)
    beta_term = jnp.einsum("td,th->dh", gathered, logit_low, preferred_element_type=jnp.float32)
    bias_term = bias_term[0]
    down_term = jnp.einsum("td,tr->dr", gathered, low_grad, preferred_element_type=jnp.float32)
    small = [up_term, down_term, beta_term, bias_term]
    packed = jnp.concatenate([term.astype(jnp.bfloat16).reshape(-1, 128) for term in small], axis=0)
    packed = lax.psum(packed, ("context", "dp")).astype(jnp.float32)
    results, start = [], 0
    for term in small:
        count = term.size // 128
        results.append(packed[start : start + count].reshape(term.shape))
        start += count
    up_grad, down_grad, beta_grad, bias_grad = results
    down_grad = lax.psum(down_grad, "head")
    input_part = jnp.einsum(
        "tr,dr->td", low_grad, down_weight, preferred_element_type=jnp.float32
    )
    input_part = input_part + jnp.einsum(
        "th,dh->td", logit_low, beta_weight, preferred_element_type=jnp.float32
    )
    input_part = input_part + jnp.einsum(
        "tc,dc->td",
        jnp.concatenate(proj_parts, axis=1),
        qkv_flat,
        preferred_element_type=jnp.float32,
    )
    input_grad = lax.psum_scatter(
        input_part.astype(jnp.bfloat16), "head", scatter_dimension=1, tiled=True
    )[None]
    return (layer_out, input_grad, qkv_grad, out_grad, up_grad, down_grad, beta_grad, bias_grad)


def solution(mesh):
    return jax.shard_map(
        shards,
        mesh=mesh,
        in_specs=(
            P("dp", "context", "head"),
            P("dp", "context", "head"),
            P(None, None, "head"),
            P(None, "head"),
            P(),
            P(None, "head"),
            P(None, "head"),
            P("head"),
        ),
        out_specs=(
            P("dp", "context", "head"),
            P("dp", "context", "head"),
            P(("context", "dp"), None, "head"),
            P(("context", "dp"), "head"),
            P(None, "head"),
            P(),
            P(None, "head"),
            P("head"),
        ),
        check_vma=False,
    )
```
